32 devices in a mesh: groups: 2 (over y), tm: 4 (over z), head: 4 (over x, core).
Axes of the slice: x: 2, y: 2, z: 4, core: 2. Of those that a mesh axis runs over, the one named last changes fastest.
Arguments:
- queries: bfloat16 [3072, 24, 128], P(('groups', 'tm'), 'head'), parts along dimension 0, may hold values from -6 to 6
- key_rows: bfloat16 [3072, 24, 128], P(('groups', 'tm'), 'head'), parts along dimension 0, may hold values from -6 to 6
- value_rows: bfloat16 [3072, 24, 128], P(('groups', 'tm'), 'head'), parts along dimension 0, may hold values from -6 to 6
- keep_tiles: int32 [24, 9], P(('groups', 'tm')), parts along dimension 0, may hold values from 0 to 1, as said below
- out_weight: bfloat16 [3072, 5120], P('head', 'tm'), may hold values from -0.109375 to 0.109375
- gate_scale: float32 [10240], P(('groups', 'head')), parts along dimension 0, may hold values from 1 to 3
Outputs:
- gated_branch: bfloat16 [3072, 5120], P(('groups', 'tm'), 'head'), parts along dimension 0
The draws below stay inside these ranges and needn't reach their ends.
There are 2 independent parts, one for each index of `groups`. The reference program is written for one: setup_inputs(seed, part) draws one part's arguments, and reference() takes and returns one part's arrays. A program takes and returns all parts, laid end to end along the dimension named above; an argument that names none is the same for every part. Nothing has to cross between parts.
Inputs may be any that keep to these rules, and one draw needn't show every extreme that they name: `keep_tiles`: each row is one query tile; the query tile itself is always kept; each row keeps 3 to 6 tiles, and some row keeps exactly 6.
All inputs are finite; a program needn't handle non-finite values.
Results may differ from the reference program's by a relative error of at most 0.014.
Values may be sent and summed in bfloat16 or wider, within the bound.
A program may use at most 64 MiB of HBM per device.

```python
import math
import jax
import jax.numpy as jnp
from jax import lax

D = 5120
HEADS = 24
HD = 128
TILE = 128
TILES_DEV = 3
KEEP_MIN = 3
KEEP_MAX = 6
TOK_DEV = 384
TOKENS = 1536
TILES = 12
REACH = 1
CAND = 9
N_TM = 4
N_HEAD = 4


def shared_rows(key, which):
    shape = (TOKENS, HEADS, HD)
    base = jax.random.normal(jax.random.fold_in(key, 11 + which), shape, jnp.float32) * 1.5
    return jnp.clip(base, -6.0, 6.0)


def draw_queries(key, part):
    return shared_rows(key, 0).astype(jnp.bfloat16)


def draw_key_rows(key, part):
    return shared_rows(key, 1).astype(jnp.bfloat16)


def draw_keep_tiles(key, part):
    counts = jax.random.randint(jax.random.fold_in(key, 1), (TILES,), KEEP_MIN, KEEP_MAX + 1)
    special = jax.random.randint(jax.random.fold_in(key, 2), (), 0, TILES)
    row_ids = jnp.arange(TILES, dtype=jnp.int32)
    counts = jnp.where(row_ids == special, KEEP_MAX, counts)
    row_keys = jax.random.split(jax.random.fold_in(key, 3), TILES)
    ranking = jax.vmap(lambda row_key: jax.random.permutation(row_key, CAND))(row_keys).astype(jnp.int32)
    own_index = REACH * TILES_DEV + row_ids % TILES_DEV
    cand_ids = jnp.arange(CAND, dtype=jnp.int32)
    own_rank = jnp.sum(jnp.where(cand_ids[None, :] == own_index[:, None], ranking, 0), axis=1)
    other_rank = ranking - (ranking > own_rank[:, None]).astype(jnp.int32)
    is_own = cand_ids[None, :] == own_index[:, None]
    kept = is_own | ~is_own & (other_rank < counts[:, None] - 1)
    return kept.astype(jnp.int32)


def shard_levels(rng, extent, cuts, smallest, top_value):
    gain, own = 1.0, jax.random.fold_in(rng, 6)
    for position, shards_of in cuts:
        heights = jnp.exp(jax.random.uniform(jax.random.fold_in(own, position), (shards_of,), jnp.float32, smallest / len(cuts), top_value / len(cuts)))
        gain = gain * jnp.repeat(heights, extent[position] // shards_of).reshape([-1 if axis == position else 1 for axis in range(len(extent))])
    return gain


def centred(rng, shape, scale, limit, pieces=(), kind=jnp.bfloat16):
    level = shard_levels(rng, shape, pieces, -0.22, 0.18) if pieces else 1.0
    values = jax.random.normal(rng, shape, jnp.float32) * scale * level
    return jnp.minimum(jnp.maximum(values, -limit), limit).astype(kind)


def setup_inputs(seed: int = 0, part: int = 0) -> dict:
    streams_of = jax.random.split(jax.random.key(seed), 7)
    own_keys = jax.random.split(jax.random.fold_in(streams_of[6], part), 7)
    queries = draw_queries(jax.random.fold_in(jax.random.fold_in(streams_of[6], part), 71), part)
    key_rows = draw_key_rows(jax.random.fold_in(jax.random.fold_in(streams_of[6], part), 71), part)
    value_rows = centred(own_keys[2], (TOKENS, HEADS, HD), 1.0, 6.0, ((0, 4), (1, 4)))
    keep_tiles = draw_keep_tiles(jax.random.fold_in(jax.random.fold_in(streams_of[6], part), 71), part)
    out_weight = centred(streams_of[4], (HEADS * HD, D), (HEADS * HD) ** -0.5, 0.109375, ((0, 4), (1, 4)))
    gate_scale = jnp.clip(1.0 + 2.0 * jax.random.uniform(own_keys[5], (D,), jnp.float32) ** shard_levels(own_keys[5], (D,), ((0, 4),), -0.2, 0.2), 1.0, 3.0)
    return {"queries": queries, "key_rows": key_rows, "value_rows": value_rows, "keep_tiles": keep_tiles, "out_weight": out_weight, "gate_scale": gate_scale}


def expand_mask(keep_rows, tile_len):
    tile_count, cand_count = keep_rows.shape
    wide = jnp.broadcast_to(keep_rows[:, None, :, None], (tile_count, tile_len, cand_count, tile_len))
    return wide.reshape(tile_count * tile_len, cand_count * tile_len)

def softmax_attend(query_block, key_block, value_block, allowed):
    score_scale = 1.0 / math.sqrt(HD)
    scores = jnp.einsum('qhd,khd->hqk', query_block.astype(jnp.float32), key_block.astype(jnp.float32)) * score_scale
    scores = jnp.where(allowed[None] > 0, scores, -jnp.inf)
    row_peak = lax.optimization_barrier(jnp.max(scores, axis=-1, keepdims=True))
    exp_scores = jnp.exp(scores - row_peak)
    row_total = lax.optimization_barrier(jnp.sum(exp_scores, axis=-1, keepdims=True))
    weights = (exp_scores / row_total).astype(jnp.bfloat16)
    attended = jnp.einsum('hqk,khd->qhd', weights.astype(jnp.float32), value_block.astype(jnp.float32))
    return attended.astype(jnp.bfloat16)

def reference(queries, key_rows, value_rows, keep_tiles, out_weight, gate_scale):
    slab_queries = queries.reshape(N_TM, TOK_DEV, HEADS, HD)
    slab_keys = key_rows.reshape(N_TM, TOK_DEV, HEADS, HD)
    slab_values = value_rows.reshape(N_TM, TOK_DEV, HEADS, HD)
    keep_slabs = keep_tiles.reshape(N_TM, TILES_DEV, CAND)
    offsets = jnp.arange(-REACH, REACH + 1, dtype=jnp.int32)

    def one_slab(slab_index):
        order = ((slab_index + offsets) % N_TM).astype(jnp.int32)
        cand_keys = jnp.take(slab_keys, order, axis=0).reshape(CAND * TILE, HEADS, HD)
        cand_values = jnp.take(slab_values, order, axis=0).reshape(CAND * TILE, HEADS, HD)
        allowed = expand_mask(keep_slabs[slab_index], TILE)
        return softmax_attend(slab_queries[slab_index], cand_keys, cand_values, allowed)
    attended = lax.map(one_slab, jnp.arange(N_TM, dtype=jnp.int32)).reshape(TOKENS, HEADS * HD)
    group_rows = HEADS * HD // N_HEAD
    projected = jnp.zeros((TOKENS, D), jnp.float32)
    for group_index in range(N_HEAD):
        lower_row = group_index * group_rows
        group_term = jnp.dot(attended[:, lower_row:lower_row + group_rows], out_weight[lower_row:lower_row + group_rows], preferred_element_type=jnp.float32)
        projected = projected + lax.optimization_barrier(group_term.astype(jnp.bfloat16)).astype(jnp.float32)
    return (gate_scale[None, :] * projected).astype(jnp.bfloat16)
```

```python
import functools
import math

import jax
import jax.numpy as jnp
from jax import lax
from jax.experimental import pallas as pl
from jax.experimental.pallas import tpu as pltpu
from jax.sharding import PartitionSpec as P

HD = 128
TILE = 128
MESH = pl.DeviceIdType.MESH


def layer_kernel(
    sizes, q_ref, k_ref, v_ref, bias_ref, w_ref, gate_ref, out_ref,
    k_all, v_all, w_all, attended, part, got,
    kv_send, kv_recv, z_send, z_recv, y_send, y_recv, r_send, r_recv, own_sem,
):
    groups, n, heads, reach, pieces = sizes
    g, t, me = lax.axis_index("groups"), lax.axis_index("tm"), lax.axis_index("head")
    rows, cols = w_ref.shape
    wide = cols // pieces
    per_head = n // heads
    part_rows = rows // groups
    tokens = q_ref.shape[0]
    slabs = 2 * reach + 1

    barrier = pltpu.get_barrier_semaphore()
    partners = []
    for d in range(1, reach + 1):
        partners += [{"tm": lax.rem(t + d, n)}, {"tm": lax.rem(t + n - d, n)}]
    for o in range(1, groups):
        partners.append({"groups": lax.rem(g + o, groups)})
    for o in range(1, heads):
        partners.append({"head": lax.rem(me + o, heads)})
    for partner in partners:
        pl.semaphore_signal(barrier, inc=1, device_id=partner, device_id_type=MESH)
    pl.semaphore_wait(barrier, len(partners))

    def remote(src, dst, send, recv, device):
        return pltpu.make_async_remote_copy(
            src_ref=src, dst_ref=dst, send_sem=send, recv_sem=recv,
            device_id=device, device_id_type=MESH,
        )

    kv_copies = []
    for d in range(1, reach + 1):
        for slot, to in ((reach - d, lax.rem(t + d, n)), (reach + d, lax.rem(t + n - d, n))):
            for which, (src, dst) in enumerate(((k_ref, k_all), (v_ref, v_all))):
                kv_copies.append(
                    remote(src, dst.at[slot], kv_send.at[slot, which], kv_recv.at[slot, which], {"tm": to})
                )
    for copy in kv_copies:
        copy.start()

    my_rows = pl.ds(pl.multiple_of(g * part_rows, part_rows), part_rows)

    def own_copy(c):
        return pltpu.make_async_copy(
            w_ref.at[:, c * wide:(c + 1) * wide], w_all.at[t, c], own_sem.at[c]
        )

    def first_send(c, side):
        to = jnp.minimum(t + 1, n - 1) if side else jnp.maximum(t - 1, 0)
        return remote(
            w_ref.at[my_rows, c * wide:(c + 1) * wide], w_all.at[t, c, my_rows],
            z_send.at[side, t, c], z_recv.at[t, c], {"tm": to},
        )

    def relay(b, c, side):
        to = jnp.minimum(t + 1, n - 1) if side else jnp.maximum(t - 1, 0)
        return remote(
            w_all.at[b, c, my_rows], w_all.at[b, c, my_rows],
            z_send.at[side, b, c], z_recv.at[b, c], {"tm": to},
        )

    def across(b, c, o):
        return remote(
            w_all.at[b, c, my_rows], w_all.at[b, c, my_rows],
            y_send.at[o - 1, b, c], y_recv.at[o - 1, b, c],
            {"groups": lax.rem(g + o, groups)},
        )

    def across_arrival(b, c, o):
        sender = lax.rem(g + groups - o, groups)
        their_rows = pl.ds(pl.multiple_of(sender * part_rows, part_rows), part_rows)
        return remote(
            w_all.at[b, c, their_rows], w_all.at[b, c, their_rows],
            y_send.at[o - 1, b, c], y_recv.at[o - 1, b, c],
            {"groups": lax.rem(g + o, groups)},
        )

    def term_send(b, c, o):
        return remote(
            part.at[b, c], got.at[o - 1, b % per_head, c],
            r_send.at[b, c], r_recv.at[o - 1, b % per_head, c],
            {"head": lax.rem(me + o, heads)},
        )

    for c in range(pieces):
        own_copy(c).start()
        @pl.when(t < n - 1)
        def _(c=c):
            first_send(c, 1).start()
        @pl.when(t > 0)
        def _(c=c):
            first_send(c, 0).start()

    for copy in kv_copies:
        copy.wait_recv()

    scale = 1.0 / math.sqrt(HD)

    def one_head(h, carry):
        lanes = pl.ds(pl.multiple_of(h * HD, HD), HD)
        for i in range(tokens // TILE):
            q = q_ref[i * TILE:(i + 1) * TILE, lanes]
            scores = []
            for j in range(slabs):
                k = k_ref[:, lanes] if j == reach else k_all[j, :, lanes]
                s = lax.dot_general(q, k, (((1,), (1,)), ((), ())), preferred_element_type=jnp.float32)
                scores.append(s * scale + bias_ref[i:i + 1, j * tokens:(j + 1) * tokens])
            peak = functools.reduce(
                jnp.maximum, [jnp.max(s, axis=1, keepdims=True) for s in scores]
            )
            exps = [jnp.exp(s - peak) for s in scores]
            total = functools.reduce(jnp.add, [jnp.sum(e, axis=1, keepdims=True) for e in exps])
            inverse = 1.0 / total
            acc = None
            for j in range(slabs):
                v = v_ref[:, lanes] if j == reach else v_all[j, :, lanes]
                term = jnp.dot(
                    (exps[j] * inverse).astype(jnp.bfloat16), v, preferred_element_type=jnp.float32
                )
                acc = term if acc is None else acc + term
            attended[i * TILE:(i + 1) * TILE, lanes] = acc.astype(jnp.bfloat16)
        return carry

    lax.fori_loop(0, q_ref.shape[1] // HD, one_head, 0)

    def project(b, c):
        def tile(i, carry):
            at = pl.ds(pl.multiple_of(i * TILE, TILE), TILE)
            part[b, c, at, :] = jnp.dot(
                attended[at, :], w_all[b, c], preferred_element_type=jnp.float32
            ).astype(jnp.bfloat16)
            return carry

        lax.fori_loop(0, tokens // TILE, tile, 0)
        owner = b // per_head
        for o in range(1, heads):
            @pl.when(owner == lax.rem(me + o, heads))
            def _():
                term_send(b, c, o).start()

    for c in range(pieces):
        own_copy(c).wait()
        project(t, c)

    items = [(c, side) for c in range(pieces) for side in (1, 0)]

    def block_of(s, side):
        return (t - 1 - s) if side else (t + 1 + s)

    def valid(s, side):
        return (t - 1 - s >= 0) if side else (t + 1 + s <= n - 1)

    def step(s, carry):
        def pass_on(c, side):
            b = block_of(s, side)
            @pl.when(valid(s, side))
            def _():
                relay(b, c, side).wait_recv()
                has_next = (t < n - 1) if side else (t > 0)
                @pl.when(has_next)
                def _():
                    relay(b, c, side).start()
                for o in range(1, groups):
                    across(b, c, o).start()

        def use(c, side):
            b = block_of(s, side)
            @pl.when(valid(s, side))
            def _():
                for o in range(1, groups):
                    across_arrival(b, c, o).wait_recv()
                project(b, c)

        last = None
        for item in items:
            pass_on(*item)
            if last is not None:
                use(*last)
            last = item
        use(*last)
        return carry

    lax.fori_loop(0, n - 1, step, 0)

    for cb in range(per_head):
        for c in range(pieces):
            b = me * per_head + cb
            for o in range(1, heads):
                term_send(b, c, o).wait_recv() if per_head == 1 else remote(
                    part.at[b, c], got.at[o - 1, cb, c], r_send.at[b, c], r_recv.at[o - 1, cb, c],
                    {"head": lax.rem(me + o, heads)},
                ).wait_recv()
            summed = part[b, c].astype(jnp.float32)
            for o in range(1, heads):
                summed = summed + got[o - 1, cb, c].astype(jnp.float32)
            at = cb * cols + c * wide
            out_ref[:, at:at + wide] = (gate_ref[:, at:at + wide] * summed).astype(out_ref.dtype)

    for copy in kv_copies:
        copy.wait_send()
    for c in range(pieces):
        @pl.when(t < n - 1)
        def _(c=c):
            first_send(c, 1).wait_send()
        @pl.when(t > 0)
        def _(c=c):
            first_send(c, 0).wait_send()

    def drain(b, carry):
        for c in range(pieces):
            @pl.when(b != t)
            def _(c=c):
                for o in range(1, groups):
                    across(b, c, o).wait_send()
            @pl.when((b < t) & (t < n - 1))
            def _(c=c):
                relay(b, c, 1).wait_send()
            @pl.when((b > t) & (t > 0))
            def _(c=c):
                relay(b, c, 0).wait_send()
            @pl.when(b // per_head != me)
            def _(c=c):
                term_send(b, c, 1).wait_send()
        return carry

    lax.fori_loop(0, n, drain, 0)


def shards(queries, key_rows, value_rows, keep_tiles, out_weight, gate_scale):
    n, heads, groups = lax.axis_size("tm"), lax.axis_size("head"), lax.axis_size("groups")
    reach = min(2, (n - 1) // 2)
    tokens = queries.shape[0]
    flat = queries.shape[1] * queries.shape[2]
    rows, cols = out_weight.shape
    pieces = 2 if cols % 256 == 0 else 1
    wide = cols // pieces
    per_head = n // heads
    slabs = 2 * reach + 1
    bias = jnp.repeat(jnp.where(keep_tiles > 0, 0.0, -jnp.inf).astype(jnp.float32), TILE, axis=1)
    vmem = pl.BlockSpec(memory_space=pltpu.VMEM)
    dma = pltpu.SemaphoreType.DMA
    bf16 = jnp.bfloat16
    return pl.pallas_call(
        functools.partial(layer_kernel, (groups, n, heads, reach, pieces)),
        out_shape=jax.ShapeDtypeStruct((tokens, gate_scale.shape[0]), bf16),
        in_specs=[vmem] * 6,
        out_specs=vmem,
        scratch_shapes=[
            pltpu.VMEM((slabs, tokens, flat), bf16),
            pltpu.VMEM((slabs, tokens, flat), bf16),
            pltpu.VMEM((n, pieces, rows, wide), bf16),
            pltpu.VMEM((tokens, flat), bf16),
            pltpu.VMEM((n, pieces, tokens, wide), bf16),
            pltpu.VMEM((heads - 1, per_head, pieces, tokens, wide), bf16),
            dma((slabs, 2)),
            dma((slabs, 2)),
            dma((2, n, pieces)),
            dma((n, pieces)),
            dma((groups - 1, n, pieces)),
            dma((groups - 1, n, pieces)),
            dma((n, pieces)),
            dma((heads - 1, per_head, pieces)),
            dma((pieces,)),
        ],
        compiler_params=pltpu.CompilerParams(
            collective_id=0, has_side_effects=True, vmem_limit_bytes=56 * 1024 * 1024
        ),
    )(
        queries.reshape(tokens, flat),
        key_rows.reshape(tokens, flat),
        value_rows.reshape(tokens, flat),
        bias,
        out_weight,
        gate_scale.reshape(1, -1),
    )


def solution(mesh):
    placed = (
        P(("groups", "tm"), "head", None),
        P(("groups", "tm"), "head", None),
        P(("groups", "tm"), "head", None),
        P(("groups", "tm"), None),
        P("head", "tm"),
        P(("groups", "head")),
    )
    return jax.shard_map(
        shards, mesh=mesh, in_specs=placed, out_specs=P(("groups", "tm"), "head"), check_vma=False
    )
```

```python
import functools
import math

import jax
import jax.numpy as jnp
from jax import lax
from jax.experimental import pallas as pl
from jax.experimental.pallas import tpu as pltpu
from jax.sharding import PartitionSpec as P

HD = 128
TILE = 128
MESH = pl.DeviceIdType.MESH


def layer_kernel(
    sizes, q_ref, k_ref, v_ref, keep_ref, w_ref, gate_ref, out_ref,
    q_own, k_all, v_all, w_all, attended, part, got,
    kv_send, kv_recv, z_send, z_recv, y_send, y_recv, r_send, r_recv, own_sem, in_sem,
):
    groups, n, heads, reach, pieces = sizes
    g, t, me = lax.axis_index("groups"), lax.axis_index("tm"), lax.axis_index("head")
    rows, cols = w_ref.shape
    wide = cols // pieces
    per_head = n // heads
    part_rows = rows // groups
    head_count, tokens = q_ref.shape[0], q_ref.shape[1]
    slabs = 2 * reach + 1

    barrier = pltpu.get_barrier_semaphore()
    partners = []
    for d in range(1, reach + 1):
        partners += [{"tm": lax.rem(t + d, n)}, {"tm": lax.rem(t + n - d, n)}]
    for o in range(1, groups):
        partners.append({"groups": lax.rem(g + o, groups)})
    for o in range(1, heads):
        partners.append({"head": lax.rem(me + o, heads)})
    for partner in partners:
        pl.semaphore_signal(barrier, inc=1, device_id=partner, device_id_type=MESH)
    pl.semaphore_wait(barrier, len(partners))

    def remote(src, dst, send, recv, device):
        return pltpu.make_async_remote_copy(
            src_ref=src, dst_ref=dst, send_sem=send, recv_sem=recv,
            device_id=device, device_id_type=MESH,
        )

    kv_copies = []
    for d in range(1, reach + 1):
        for slot, to in ((reach - d, lax.rem(t + d, n)), (reach + d, lax.rem(t + n - d, n))):
            for which, (src, dst) in enumerate(((k_ref, k_all), (v_ref, v_all))):
                kv_copies.append(
                    remote(src, dst.at[slot], kv_send.at[slot, which], kv_recv.at[slot, which], {"tm": to})
                )
    for copy in kv_copies:
        copy.start()
    in_copies = [
        pltpu.make_async_copy(src, dst, in_sem.at[i])
        for i, (src, dst) in enumerate(
            ((q_ref, q_own), (k_ref, k_all.at[reach]), (v_ref, v_all.at[reach]))
        )
    ]
    for copy in in_copies:
        copy.start()

    my_rows = pl.ds(pl.multiple_of(g * part_rows, part_rows), part_rows)

    def own_copy(c):
        return pltpu.make_async_copy(
            w_ref.at[:, c * wide:(c + 1) * wide], w_all.at[t, c], own_sem.at[c]
        )

    def first_send(c, side):
        to = jnp.minimum(t + 1, n - 1) if side else jnp.maximum(t - 1, 0)
        return remote(
            w_ref.at[my_rows, c * wide:(c + 1) * wide], w_all.at[t, c, my_rows],
            z_send.at[side, t, c], z_recv.at[t, c], {"tm": to},
        )

    def relay(b, c, side):
        to = jnp.minimum(t + 1, n - 1) if side else jnp.maximum(t - 1, 0)
        return remote(
            w_all.at[b, c, my_rows], w_all.at[b, c, my_rows],
            z_send.at[side, b, c], z_recv.at[b, c], {"tm": to},
        )

    def across(b, c, o):
        return remote(
            w_all.at[b, c, my_rows], w_all.at[b, c, my_rows],
            y_send.at[o - 1, b, c], y_recv.at[o - 1, b, c],
            {"groups": lax.rem(g + o, groups)},
        )

    def across_arrival(b, c, o):
        sender = lax.rem(g + groups - o, groups)
        their_rows = pl.ds(pl.multiple_of(sender * part_rows, part_rows), part_rows)
        return remote(
            w_all.at[b, c, their_rows], w_all.at[b, c, their_rows],
            y_send.at[o - 1, b, c], y_recv.at[o - 1, b, c],
            {"groups": lax.rem(g + o, groups)},
        )

    def term_send(b, c, o):
        return remote(
            part.at[b, c], got.at[o - 1, b % per_head, c],
            r_send.at[b, c], r_recv.at[o - 1, b % per_head, c],
            {"head": lax.rem(me + o, heads)},
        )

    for c in range(pieces):
        own_copy(c).start()
        @pl.when(t < n - 1)
        def _(c=c):
            first_send(c, 1).start()
        @pl.when(t > 0)
        def _(c=c):
            first_send(c, 0).start()

    for copy in in_copies:
        copy.wait()
    for copy in kv_copies:
        copy.wait_recv()

    scale = 1.0 / math.sqrt(HD)
    per_slab = tokens // TILE

    def one_head(h, carry):
        lanes = pl.ds(pl.multiple_of(h * HD, HD), HD)
        for i in range(per_slab):
            q = q_own[h, i * TILE:(i + 1) * TILE, :]
            scores = []
            for j in range(slabs):
                s = lax.dot_general(
                    q, k_all[j, h], (((1,), (1,)), ((), ())), preferred_element_type=jnp.float32
                )
                bias = jnp.concatenate(
                    [
                        jnp.full(
                            (1, TILE),
                            jnp.where(keep_ref[i, j * per_slab + u] > 0, 0.0, -jnp.inf),
                            jnp.float32,
                        )
                        for u in range(per_slab)
                    ],
                    axis=1,
                )
                scores.append(s * scale + bias)
            peak = functools.reduce(
                jnp.maximum, [jnp.max(s, axis=1, keepdims=True) for s in scores]
            )
            exps = [jnp.exp(s - peak) for s in scores]
            total = functools.reduce(jnp.add, [jnp.sum(e, axis=1, keepdims=True) for e in exps])
            inverse = 1.0 / total
            acc = None
            for j in range(slabs):
                term = jnp.dot(
                    (exps[j] * inverse).astype(jnp.bfloat16), v_all[j, h],
                    preferred_element_type=jnp.float32,
                )
                acc = term if acc is None else acc + term
            attended[i * TILE:(i + 1) * TILE, lanes] = acc.astype(jnp.bfloat16)
        return carry

    lax.fori_loop(0, head_count, one_head, 0)

    def project(b, c):
        def tile(i, carry):
            at = pl.ds(pl.multiple_of(i * TILE, TILE), TILE)
            part[b, c, at, :] = jnp.dot(
                attended[at, :], w_all[b, c], preferred_element_type=jnp.float32
            ).astype(jnp.bfloat16)
            return carry

        lax.fori_loop(0, tokens // TILE, tile, 0)
        owner = b // per_head
        for o in range(1, heads):
            @pl.when(owner == lax.rem(me + o, heads))
            def _():
                term_send(b, c, o).start()

    for c in range(pieces):
        own_copy(c).wait()
        project(t, c)

    def pass_on(j, side):
        step, c = j // pieces, j % pieces
        b = (t - 1 - step) if side else (t + 1 + step)
        @pl.when((b >= 0) & (b <= n - 1))
        def _():
            relay(b, c, side).wait_recv()
            @pl.when((t < n - 1) if side else (t > 0))
            def _():
                relay(b, c, side).start()
            for o in range(1, groups):
                across(b, c, o).start()

    def use(j, side):
        step, c = j // pieces, j % pieces
        b = (t - 1 - step) if side else (t + 1 + step)
        @pl.when((b >= 0) & (b <= n - 1))
        def _():
            for o in range(1, groups):
                across_arrival(b, c, o).wait_recv()
            project(b, c)

    def step(j, carry):
        for side in (1, 0):
            pass_on(j, side)
        @pl.when(j > 0)
        def _():
            for side in (1, 0):
                use(j - 1, side)
        return carry

    count = (n - 1) * pieces
    lax.fori_loop(0, count, step, 0)
    for side in (1, 0):
        use(count - 1, side)

    for cb in range(per_head):
        for c in range(pieces):
            b = me * per_head + cb
            for o in range(1, heads):
                term_send(b, c, o).wait_recv()
            span = wide if gate_ref.shape[0] == 1 else gate_ref.shape[1]
            for u in range(wide // span):
                lanes = slice(u * span, (u + 1) * span)
                summed = part[b, c, :, lanes].astype(jnp.float32)
                for o in range(1, heads):
                    summed = summed + got[o - 1, cb, c, :, lanes].astype(jnp.float32)
                at = cb * cols + c * wide + u * span
                gate = gate_ref[:, at:at + span] if span == wide else gate_ref[at // span:at // span + 1, :]
                out_ref[:, at:at + span] = (gate * summed).astype(out_ref.dtype)

    for copy in kv_copies:
        copy.wait_send()
    for c in range(pieces):
        @pl.when(t < n - 1)
        def _(c=c):
            first_send(c, 1).wait_send()
        @pl.when(t > 0)
        def _(c=c):
            first_send(c, 0).wait_send()

    def drain(b, carry):
        for c in range(pieces):
            @pl.when(b != t)
            def _(c=c):
                for o in range(1, groups):
                    across(b, c, o).wait_send()
            @pl.when((b < t) & (t < n - 1))
            def _(c=c):
                relay(b, c, 1).wait_send()
            @pl.when((b > t) & (t > 0))
            def _(c=c):
                relay(b, c, 0).wait_send()
            @pl.when(b // per_head != me)
            def _(c=c):
                term_send(b, c, 1).wait_send()
        return carry

    lax.fori_loop(0, n, drain, 0)


def shards(queries, key_rows, value_rows, keep_tiles, out_weight, gate_scale):
    n, heads, groups = lax.axis_size("tm"), lax.axis_size("head"), lax.axis_size("groups")
    reach = min(2, (n - 1) // 2)
    tokens = queries.shape[0]
    head_count = queries.shape[1]
    flat = head_count * HD
    rows, cols = out_weight.shape
    pieces = cols // 256 if cols % 256 == 0 else 1
    wide = cols // pieces
    per_head = n // heads
    slabs = 2 * reach + 1
    gate_lanes = 128 if wide % 128 == 0 else gate_scale.shape[0]
    vmem = pl.BlockSpec(memory_space=pltpu.VMEM)
    hbm = pl.BlockSpec(memory_space=pl.ANY)
    dma = pltpu.SemaphoreType.DMA
    bf16 = jnp.bfloat16
    return pl.pallas_call(
        functools.partial(layer_kernel, (groups, n, heads, reach, pieces)),
        out_shape=jax.ShapeDtypeStruct((tokens, gate_scale.shape[0]), bf16),
        in_specs=[hbm, hbm, hbm, pl.BlockSpec(memory_space=pltpu.SMEM), hbm, vmem],
        out_specs=vmem,
        scratch_shapes=[
            pltpu.VMEM((head_count, tokens, HD), bf16),
            pltpu.VMEM((slabs, head_count, tokens, HD), bf16),
            pltpu.VMEM((slabs, head_count, tokens, HD), bf16),
            pltpu.VMEM((n, pieces, rows, wide), bf16),
            pltpu.VMEM((tokens, flat), bf16),
            pltpu.VMEM((n, pieces, tokens, wide), bf16),
            pltpu.VMEM((heads - 1, per_head, pieces, tokens, wide), bf16),
            dma((slabs, 2)),
            dma((slabs, 2)),
            dma((2, n, pieces)),
            dma((n, pieces)),
            dma((groups - 1, n, pieces)),
            dma((groups - 1, n, pieces)),
            dma((n, pieces)),
            dma((heads - 1, per_head, pieces)),
            dma((pieces,)),
            dma((3,)),
        ],
        compiler_params=pltpu.CompilerParams(
            collective_id=0, has_side_effects=True, vmem_limit_bytes=56 * 1024 * 1024
        ),
    )(
        queries.transpose(1, 0, 2),
        key_rows.transpose(1, 0, 2),
        value_rows.transpose(1, 0, 2),
        keep_tiles,
        out_weight,
        gate_scale.reshape(-1, gate_lanes),
    )


def solution(mesh):
    placed = (
        P(("groups", "tm"), "head", None),
        P(("groups", "tm"), "head", None),
        P(("groups", "tm"), "head", None),
        P(("groups", "tm"), None),
        P("head", "tm"),
        P(("groups", "head")),
    )
    return jax.shard_map(
        shards, mesh=mesh, in_specs=placed, out_specs=P(("groups", "tm"), "head"), check_vma=False
    )
```

```python
import functools
import math

import jax
import jax.numpy as jnp
from jax import lax
from jax.experimental import pallas as pl
from jax.experimental.pallas import tpu as pltpu
from jax.sharding import PartitionSpec as P

HD = 128
TILE = 128
MESH = pl.DeviceIdType.MESH


def layer_kernel(
    sizes, q_ref, k_ref, v_ref, keep_ref, w_ref, gate_ref, out_ref,
    q_own, k_all, v_all, w_all, attended, part, got,
    kv_send, kv_recv, z_send, z_recv, y_send, y_recv, r_send, r_recv, own_sem, in_sem,
):
    groups, n, heads, reach, pieces = sizes
    g, t, me = lax.axis_index("groups"), lax.axis_index("tm"), lax.axis_index("head")
    rows, cols = w_ref.shape
    wide = cols // pieces
    per_head = n // heads
    part_rows = rows // groups
    head_count, tokens = q_ref.shape[0], q_ref.shape[1]
    slabs = 2 * reach + 1

    barrier = pltpu.get_barrier_semaphore()
    partners = []
    for d in range(1, reach + 1):
        partners += [{"tm": lax.rem(t + d, n)}, {"tm": lax.rem(t + n - d, n)}]
    for o in range(1, groups):
        partners.append({"groups": lax.rem(g + o, groups)})
    for o in range(1, heads):
        partners.append({"head": lax.rem(me + o, heads)})
    for partner in partners:
        pl.semaphore_signal(barrier, inc=1, device_id=partner, device_id_type=MESH)
    pl.semaphore_wait(barrier, len(partners))

    def remote(src, dst, send, recv, device):
        return pltpu.make_async_remote_copy(
            src_ref=src, dst_ref=dst, send_sem=send, recv_sem=recv,
            device_id=device, device_id_type=MESH,
        )

    kv_copies = []
    for d in range(1, reach + 1):
        for slot, to in ((reach - d, lax.rem(t + d, n)), (reach + d, lax.rem(t + n - d, n))):
            for which, (src, dst) in enumerate(((k_ref, k_all), (v_ref, v_all))):
                kv_copies.append(
                    remote(src, dst.at[slot], kv_send.at[slot, which], kv_recv.at[slot, which], {"tm": to})
                )
    for copy in kv_copies:
        copy.start()
    in_copies = [
        pltpu.make_async_copy(src, dst, in_sem.at[i])
        for i, (src, dst) in enumerate(
            ((q_ref, q_own), (k_ref, k_all.at[reach]), (v_ref, v_all.at[reach]))
        )
    ]
    for copy in in_copies:
        copy.start()

    my_rows = pl.ds(pl.multiple_of(g * part_rows, part_rows), part_rows)

    def own_copy(c):
        return pltpu.make_async_copy(
            w_ref.at[:, c * wide:(c + 1) * wide], w_all.at[t, c], own_sem.at[c]
        )

    def first_send(c, side):
        to = jnp.minimum(t + 1, n - 1) if side else jnp.maximum(t - 1, 0)
        return remote(
            w_ref.at[my_rows, c * wide:(c + 1) * wide], w_all.at[t, c, my_rows],
            z_send.at[side, t, c], z_recv.at[t, c], {"tm": to},
        )

    def relay(b, c, side):
        to = jnp.minimum(t + 1, n - 1) if side else jnp.maximum(t - 1, 0)
        return remote(
            w_all.at[b, c, my_rows], w_all.at[b, c, my_rows],
            z_send.at[side, b, c], z_recv.at[b, c], {"tm": to},
        )

    def across(b, c, o):
        return remote(
            w_all.at[b, c, my_rows], w_all.at[b, c, my_rows],
            y_send.at[o - 1, b, c], y_recv.at[o - 1, b, c],
            {"groups": lax.rem(g + o, groups)},
        )

    def across_arrival(b, c, o):
        sender = lax.rem(g + groups - o, groups)
        their_rows = pl.ds(pl.multiple_of(sender * part_rows, part_rows), part_rows)
        return remote(
            w_all.at[b, c, their_rows], w_all.at[b, c, their_rows],
            y_send.at[o - 1, b, c], y_recv.at[o - 1, b, c],
            {"groups": lax.rem(g + o, groups)},
        )

    def term_send(b, c, o):
        return remote(
            part.at[b, c], got.at[o - 1, b % per_head, c],
            r_send.at[b, c], r_recv.at[o - 1, b % per_head, c],
            {"head": lax.rem(me + o, heads)},
        )

    for c in range(pieces):
        own_copy(c).start()
        @pl.when(t < n - 1)
        def _(c=c):
            first_send(c, 1).start()
        @pl.when(t > 0)
        def _(c=c):
            first_send(c, 0).start()

    for copy in in_copies:
        copy.wait()
    for copy in kv_copies:
        copy.wait_recv()

    scale = 1.0 / math.sqrt(HD)
    per_slab = tokens // TILE

    early = min(pieces, head_count - 1)

    def pass_on(j, side):
        step, c = j // pieces, j % pieces
        b = (t - 1 - step) if side else (t + 1 + step)
        @pl.when((b >= 0) & (b <= n - 1))
        def _():
            relay(b, c, side).wait_recv()
            @pl.when((t < n - 1) if side else (t > 0))
            def _():
                relay(b, c, side).start()
            for o in range(1, groups):
                across(b, c, o).start()

    def one_head(h, carry):
        lanes = pl.ds(pl.multiple_of(h * HD, HD), HD)
        for i in range(per_slab):
            q = q_own[h, i * TILE:(i + 1) * TILE, :]
            scores = []
            for j in range(slabs):
                s = lax.dot_general(
                    q, k_all[j, h], (((1,), (1,)), ((), ())), preferred_element_type=jnp.float32
                )
                bias = jnp.concatenate(
                    [
                        jnp.full(
                            (1, TILE),
                            jnp.where(keep_ref[i, j * per_slab + u] > 0, 0.0, -jnp.inf),
                            jnp.float32,
                        )
                        for u in range(per_slab)
                    ],
                    axis=1,
                )
                scores.append(s * scale + bias)
            peak = functools.reduce(
                jnp.maximum, [jnp.max(s, axis=1, keepdims=True) for s in scores]
            )
            exps = [jnp.exp(s - peak) for s in scores]
            total = functools.reduce(jnp.add, [jnp.sum(e, axis=1, keepdims=True) for e in exps])
            inverse = 1.0 / total
            acc = None
            for j in range(slabs):
                term = jnp.dot(
                    (exps[j] * inverse).astype(jnp.bfloat16), v_all[j, h],
                    preferred_element_type=jnp.float32,
                )
                acc = term if acc is None else acc + term
            attended[i * TILE:(i + 1) * TILE, lanes] = acc.astype(jnp.bfloat16)
        @pl.when(h >= head_count - early)
        def _():
            for side in (1, 0):
                pass_on(h - (head_count - early), side)
        return carry

    lax.fori_loop(0, head_count, one_head, 0)

    def project(b, c):
        def tile(i, carry):
            at = pl.ds(pl.multiple_of(i * TILE, TILE), TILE)
            part[b, c, at, :] = jnp.dot(
                attended[at, :], w_all[b, c], preferred_element_type=jnp.float32
            ).astype(jnp.bfloat16)
            return carry

        lax.fori_loop(0, tokens // TILE, tile, 0)
        owner = b // per_head
        for o in range(1, heads):
            @pl.when(owner == lax.rem(me + o, heads))
            def _():
                term_send(b, c, o).start()

    for c in range(pieces):
        own_copy(c).wait()
        project(t, c)

    def use(j, side):
        step, c = j // pieces, j % pieces
        b = (t - 1 - step) if side else (t + 1 + step)
        @pl.when((b >= 0) & (b <= n - 1))
        def _():
            for o in range(1, groups):
                across_arrival(b, c, o).wait_recv()
            project(b, c)

    def step(j, carry):
        @pl.when(j >= early)
        def _():
            for side in (1, 0):
                pass_on(j, side)
        @pl.when(j > 0)
        def _():
            for side in (1, 0):
                use(j - 1, side)
        return carry

    count = (n - 1) * pieces
    lax.fori_loop(0, count, step, 0)
    for side in (1, 0):
        use(count - 1, side)

    for cb in range(per_head):
        for c in range(pieces):
            b = me * per_head + cb
            for o in range(1, heads):
                term_send(b, c, o).wait_recv()
            span = wide if gate_ref.shape[0] == 1 else gate_ref.shape[1]
            for u in range(wide // span):
                lanes = slice(u * span, (u + 1) * span)
                summed = part[b, c, :, lanes].astype(jnp.float32)
                for o in range(1, heads):
                    summed = summed + got[o - 1, cb, c, :, lanes].astype(jnp.float32)
                at = cb * cols + c * wide + u * span
                gate = gate_ref[:, at:at + span] if span == wide else gate_ref[at // span:at // span + 1, :]
                out_ref[:, at:at + span] = (gate * summed).astype(out_ref.dtype)

    for copy in kv_copies:
        copy.wait_send()
    for c in range(pieces):
        @pl.when(t < n - 1)
        def _(c=c):
            first_send(c, 1).wait_send()
        @pl.when(t > 0)
        def _(c=c):
            first_send(c, 0).wait_send()

    def drain(b, carry):
        for c in range(pieces):
            @pl.when(b != t)
            def _(c=c):
                for o in range(1, groups):
                    across(b, c, o).wait_send()
            @pl.when((b < t) & (t < n - 1))
            def _(c=c):
                relay(b, c, 1).wait_send()
            @pl.when((b > t) & (t > 0))
            def _(c=c):
                relay(b, c, 0).wait_send()
            @pl.when(b // per_head != me)
            def _(c=c):
                term_send(b, c, 1).wait_send()
        return carry

    lax.fori_loop(0, n, drain, 0)


def shards(queries, key_rows, value_rows, keep_tiles, out_weight, gate_scale):
    n, heads, groups = lax.axis_size("tm"), lax.axis_size("head"), lax.axis_size("groups")
    reach = min(2, (n - 1) // 2)
    tokens = queries.shape[0]
    head_count = queries.shape[1]
    flat = head_count * HD
    rows, cols = out_weight.shape
    pieces = cols // 256 if cols % 256 == 0 else 1
    wide = cols // pieces
    per_head = n // heads
    slabs = 2 * reach + 1
    gate_lanes = 128 if wide % 128 == 0 else gate_scale.shape[0]
    vmem = pl.BlockSpec(memory_space=pltpu.VMEM)
    hbm = pl.BlockSpec(memory_space=pl.ANY)
    dma = pltpu.SemaphoreType.DMA
    bf16 = jnp.bfloat16
    return pl.pallas_call(
        functools.partial(layer_kernel, (groups, n, heads, reach, pieces)),
        out_shape=jax.ShapeDtypeStruct((tokens, gate_scale.shape[0]), bf16),
        in_specs=[hbm, hbm, hbm, pl.BlockSpec(memory_space=pltpu.SMEM), hbm, vmem],
        out_specs=vmem,
        scratch_shapes=[
            pltpu.VMEM((head_count, tokens, HD), bf16),
            pltpu.VMEM((slabs, head_count, tokens, HD), bf16),
            pltpu.VMEM((slabs, head_count, tokens, HD), bf16),
            pltpu.VMEM((n, pieces, rows, wide), bf16),
            pltpu.VMEM((tokens, flat), bf16),
            pltpu.VMEM((n, pieces, tokens, wide), bf16),
            pltpu.VMEM((heads - 1, per_head, pieces, tokens, wide), bf16),
            dma((slabs, 2)),
            dma((slabs, 2)),
            dma((2, n, pieces)),
            dma((n, pieces)),
            dma((groups - 1, n, pieces)),
            dma((groups - 1, n, pieces)),
            dma((n, pieces)),
            dma((heads - 1, per_head, pieces)),
            dma((pieces,)),
            dma((3,)),
        ],
        compiler_params=pltpu.CompilerParams(
            collective_id=0, has_side_effects=True, vmem_limit_bytes=56 * 1024 * 1024
        ),
    )(
        queries.transpose(1, 0, 2),
        key_rows.transpose(1, 0, 2),
        value_rows.transpose(1, 0, 2),
        keep_tiles,
        out_weight,
        gate_scale.reshape(-1, gate_lanes),
    )


def solution(mesh):
    placed = (
        P(("groups", "tm"), "head", None),
        P(("groups", "tm"), "head", None),
        P(("groups", "tm"), "head", None),
        P(("groups", "tm"), None),
        P("head", "tm"),
        P(("groups", "head")),
    )
    return jax.shard_map(
        shards, mesh=mesh, in_specs=placed, out_specs=P(("groups", "tm"), "head"), check_vma=False
    )
```

```python
import functools
import math

import jax
import jax.numpy as jnp
from jax import lax
from jax.experimental import pallas as pl
from jax.experimental.pallas import tpu as pltpu
from jax.sharding import PartitionSpec as P

HD = 128
TILE = 128
MESH = pl.DeviceIdType.MESH


def layer_kernel(
    sizes, q_ref, k_ref, v_ref, keep_ref, w_ref, gate_ref, out_ref,
    q_own, k_all, v_all, w_all, attended, part, got,
    kv_send, kv_recv, z_send, z_recv, y_send, y_recv, r_send, r_recv, own_sem, in_sem,
    q_far, o_far, o_in, bias_out, bias_in, stats_far, stats_in, stats_own, f_send, f_recv,
):
    groups, n, heads, reach, pieces = sizes
    g, t, me = lax.axis_index("groups"), lax.axis_index("tm"), lax.axis_index("head")
    rows, cols = w_ref.shape
    wide = cols // pieces
    per_head = n // heads
    part_rows = rows // groups
    head_count, tokens = q_ref.shape[0], q_ref.shape[1]
    slabs = 2 * reach + 1

    fold = reach == 1 and n == 4
    per_slab = tokens // TILE
    is_end = (t == 0) | (t == n - 1)
    is_helper = (t == 1) | (t == n - 2)
    end_helper = jnp.where(t == 0, 1, n - 2)
    peer = jnp.where(is_end, end_helper, jnp.where(t == 1, 0, n - 1))

    def keep_bias(i, j):
        return [
            jnp.where(keep_ref[i, j * per_slab + u] > 0, 0.0, -jnp.inf) for u in range(per_slab)
        ]

    def bias_row(values):
        return jnp.concatenate([jnp.full((1, TILE), x, jnp.float32) for x in values], axis=1)

    if fold:
        bias_out[...] = jnp.zeros_like(bias_out)
        for i in range(per_slab):
            bias_out[i:i + 1, :] = bias_row(
                [jnp.where(t == 0, a, b) for a, b in zip(keep_bias(i, 0), keep_bias(i, 2))]
            )

    barrier = pltpu.get_barrier_semaphore()
    partners = []
    for d in range(1, reach + 1):
        partners += [{"tm": lax.rem(t + d, n)}, {"tm": lax.rem(t + n - d, n)}]
    if fold:
        partners.append({"tm": lax.rem(t + 2, n)})
    for o in range(1, groups):
        partners.append({"groups": lax.rem(g + o, groups)})
    for o in range(1, heads):
        partners.append({"head": lax.rem(me + o, heads)})
    for partner in partners:
        pl.semaphore_signal(barrier, inc=1, device_id=partner, device_id_type=MESH)
    pl.semaphore_wait(barrier, len(partners))

    def remote(src, dst, send, recv, device):
        return pltpu.make_async_remote_copy(
            src_ref=src, dst_ref=dst, send_sem=send, recv_sem=recv,
            device_id=device, device_id_type=MESH,
        )

    kv_copies = []
    kv_arrivals = []
    for d in range(1, reach + 1):
        for slot, to, wraps, absent in (
            (reach - d, lax.rem(t + d, n), t == n - 1, t == 0),
            (reach + d, lax.rem(t + n - d, n), t == 0, t == n - 1),
        ):
            target, place = to, slot
            if fold:
                target = jnp.where(wraps, lax.rem(t + 2, n), to)
                place = jnp.where(wraps, slabs, slot)
            for which, (src, dst) in enumerate(((k_ref, k_all), (v_ref, v_all))):
                kv_copies.append(
                    remote(
                        src, dst.at[place], kv_send.at[slot, which], kv_recv.at[place, which],
                        {"tm": target},
                    )
                )
                kv_arrivals.append((
                    remote(
                        src, dst.at[slot], kv_send.at[slot, which], kv_recv.at[slot, which],
                        {"tm": to},
                    ),
                    absent,
                    pltpu.make_async_copy(src, dst.at[slot], in_sem.at[3 + which]),
                ))
    in_copies = [
        pltpu.make_async_copy(src, dst, in_sem.at[i])
        for i, (src, dst) in enumerate(
            ((q_ref, q_own), (k_ref, k_all.at[reach]), (v_ref, v_all.at[reach]))
        )
    ]
    if fold:
        out_copies = [
            remote(src, dst, f_send.at[i], f_recv.at[i], {"tm": peer})
            for i, (src, dst) in enumerate(((q_ref, q_far), (bias_out, bias_in)))
        ]
        back_copies = [
            remote(src, dst, f_send.at[2 + i], f_recv.at[2 + i], {"tm": peer})
            for i, (src, dst) in enumerate(((o_far, o_in), (stats_far, stats_in)))
        ]
        far_arrivals = [
            remote(src, dst.at[slabs], kv_send.at[0, i], kv_recv.at[slabs, i], {"tm": peer})
            for i, (src, dst) in enumerate(((k_ref, k_all), (v_ref, v_all)))
        ]

        @pl.when(is_end)
        def _():
            for copy in out_copies:
                copy.start()

        @pl.when(t == 0)
        def _():
            for copy in kv_copies[2:] + kv_copies[:2]:
                copy.start()

        @pl.when(t != 0)
        def _():
            for copy in kv_copies:
                copy.start()
    else:
        for copy in kv_copies:
            copy.start()
    for copy in in_copies:
        copy.start()

    my_rows = pl.ds(pl.multiple_of(g * part_rows, part_rows), part_rows)

    def own_copy(c):
        return pltpu.make_async_copy(
            w_ref.at[:, c * wide:(c + 1) * wide], w_all.at[t, c], own_sem.at[c]
        )

    def first_send(c, side):
        to = jnp.minimum(t + 1, n - 1) if side else jnp.maximum(t - 1, 0)
        return remote(
            w_ref.at[my_rows, c * wide:(c + 1) * wide], w_all.at[t, c, my_rows],
            z_send.at[side, t, c], z_recv.at[t, c], {"tm": to},
        )

    def relay(b, c, side):
        to = jnp.minimum(t + 1, n - 1) if side else jnp.maximum(t - 1, 0)
        return remote(
            w_all.at[b, c, my_rows], w_all.at[b, c, my_rows],
            z_send.at[side, b, c], z_recv.at[b, c], {"tm": to},
        )

    def across(b, c, o):
        return remote(
            w_all.at[b, c, my_rows], w_all.at[b, c, my_rows],
            y_send.at[o - 1, b, c], y_recv.at[o - 1, b, c],
            {"groups": lax.rem(g + o, groups)},
        )

    def across_arrival(b, c, o):
        sender = lax.rem(g + groups - o, groups)
        their_rows = pl.ds(pl.multiple_of(sender * part_rows, part_rows), part_rows)
        return remote(
            w_all.at[b, c, their_rows], w_all.at[b, c, their_rows],
            y_send.at[o - 1, b, c], y_recv.at[o - 1, b, c],
            {"groups": lax.rem(g + o, groups)},
        )

    def term_send(b, c, o):
        return remote(
            part.at[b, c], got.at[o - 1, b % per_head, c],
            r_send.at[b, c], r_recv.at[o - 1, b % per_head, c],
            {"head": lax.rem(me + o, heads)},
        )

    for c in range(pieces):
        own_copy(c).start()
        @pl.when(t < n - 1)
        def _(c=c):
            first_send(c, 1).start()
        @pl.when(t > 0)
        def _(c=c):
            first_send(c, 0).start()

    for copy in in_copies:
        copy.wait()
    for copy, absent, filler in kv_arrivals:
        if not fold:
            copy.wait_recv()
            continue

        @pl.when(absent)
        def _(filler=filler):
            filler.start()
            filler.wait()

        @pl.when(jnp.logical_not(absent))
        def _(copy=copy):
            copy.wait_recv()

    scale = 1.0 / math.sqrt(HD)
    lane_ids = lax.broadcasted_iota(jnp.int32, (TILE, 128), 1)

    def keep_stats(stats, i, h, peak, total):
        at = slice(i * TILE, (i + 1) * TILE)
        stats[at, :] = jnp.where(
            lane_ids == h, peak, jnp.where(lane_ids == h + 64, total, stats[at, :])
        )

    def far_head(h, carry):
        for i in range(per_slab):
            at = slice(i * TILE, (i + 1) * TILE)
            s = lax.dot_general(
                q_far[h, at, :], k_all[slabs, h], (((1,), (1,)), ((), ())),
                preferred_element_type=jnp.float32,
            ) * scale + bias_in[i:i + 1, :]
            peak = jnp.maximum(jnp.max(s, axis=1, keepdims=True), -1e30)
            e = jnp.exp(s - peak)
            keep_stats(stats_far, i, h, peak, jnp.sum(e, axis=1, keepdims=True))
            o_far[h, at, :] = jnp.dot(
                e.astype(jnp.bfloat16), v_all[slabs, h], preferred_element_type=jnp.float32
            ).astype(jnp.bfloat16)
        return carry

    if fold:
        @pl.when(is_helper)
        def _():
            stats_far[...] = jnp.zeros_like(stats_far)
            for copy in far_arrivals + out_copies:
                copy.wait_recv()
            lax.fori_loop(0, head_count, far_head, 0)
            for copy in back_copies:
                copy.start()

        stats_own[...] = jnp.zeros_like(stats_own)

    early = min(pieces, head_count - 1)

    def pass_on(j, side):
        step, c = j // pieces, j % pieces
        b = (t - 1 - step) if side else (t + 1 + step)
        @pl.when((b >= 0) & (b <= n - 1))
        def _():
            relay(b, c, side).wait_recv()
            @pl.when((t < n - 1) if side else (t > 0))
            def _():
                relay(b, c, side).start()
            for o in range(1, groups):
                across(b, c, o).start()

    def one_head(h, carry):
        lanes = pl.ds(pl.multiple_of(h * HD, HD), HD)
        for i in range(per_slab):
            q = q_own[h, i * TILE:(i + 1) * TILE, :]
            scores = []
            for j in range(slabs):
                s = lax.dot_general(
                    q, k_all[j, h], (((1,), (1,)), ((), ())), preferred_element_type=jnp.float32
                )
                values = keep_bias(i, j)
                if fold and j != reach:
                    absent = t == (0 if j < reach else n - 1)
                    values = [jnp.where(absent, -jnp.inf, x) for x in values]
                bias = bias_row(values)
                scores.append(s * scale + bias)
            peak = functools.reduce(
                jnp.maximum, [jnp.max(s, axis=1, keepdims=True) for s in scores]
            )
            exps = [jnp.exp(s - peak) for s in scores]
            total = functools.reduce(jnp.add, [jnp.sum(e, axis=1, keepdims=True) for e in exps])
            inverse = 1.0 / total
            if fold:
                keep_stats(stats_own, i, h, peak, total)
            acc = None
            for j in range(slabs):
                term = jnp.dot(
                    (exps[j] * inverse).astype(jnp.bfloat16), v_all[j, h],
                    preferred_element_type=jnp.float32,
                )
                acc = term if acc is None else acc + term
            attended[i * TILE:(i + 1) * TILE, lanes] = acc.astype(jnp.bfloat16)
        @pl.when(h >= head_count - early)
        def _():
            for side in (1, 0):
                pass_on(h - (head_count - early), side)
        return carry

    lax.fori_loop(0, head_count, one_head, 0)

    def merge_head(h, carry):
        lanes = pl.ds(pl.multiple_of(h * HD, HD), HD)
        for i in range(per_slab):
            at = slice(i * TILE, (i + 1) * TILE)

            def column(stats, lane):
                return jnp.sum(
                    jnp.where(lane_ids == lane, stats[at, :], 0.0), axis=1, keepdims=True
                )

            peak, total = column(stats_own, h), column(stats_own, h + 64)
            far_peak, far_total = column(stats_in, h), column(stats_in, h + 64)
            top = jnp.maximum(peak, far_peak)
            near = total * jnp.exp(peak - top)
            far = jnp.exp(far_peak - top)
            inverse = 1.0 / (near + far_total * far)
            attended[at, lanes] = (
                attended[at, lanes].astype(jnp.float32) * (near * inverse)
                + o_in[h, at, :].astype(jnp.float32) * (far * inverse)
            ).astype(jnp.bfloat16)
        return carry

    if fold:
        @pl.when(is_end)
        def _():
            for copy in back_copies:
                copy.wait_recv()
            lax.fori_loop(0, head_count, merge_head, 0)

    def project(b, c):
        def tile(i, carry):
            at = pl.ds(pl.multiple_of(i * TILE, TILE), TILE)
            part[b, c, at, :] = jnp.dot(
                attended[at, :], w_all[b, c], preferred_element_type=jnp.float32
            ).astype(jnp.bfloat16)
            return carry

        lax.fori_loop(0, tokens // TILE, tile, 0)
        owner = b // per_head
        for o in range(1, heads):
            @pl.when(owner == lax.rem(me + o, heads))
            def _():
                term_send(b, c, o).start()

    for c in range(pieces):
        own_copy(c).wait()
        project(t, c)

    def use(j, side):
        step, c = j // pieces, j % pieces
        b = (t - 1 - step) if side else (t + 1 + step)
        @pl.when((b >= 0) & (b <= n - 1))
        def _():
            for o in range(1, groups):
                across_arrival(b, c, o).wait_recv()
            project(b, c)

    def step(j, carry):
        @pl.when(j >= early)
        def _():
            for side in (1, 0):
                pass_on(j, side)
        @pl.when(j > 0)
        def _():
            for side in (1, 0):
                use(j - 1, side)
        return carry

    count = (n - 1) * pieces
    lax.fori_loop(0, count, step, 0)
    for side in (1, 0):
        use(count - 1, side)

    for cb in range(per_head):
        for c in range(pieces):
            b = me * per_head + cb
            for o in range(1, heads):
                term_send(b, c, o).wait_recv()
            span = wide if gate_ref.shape[0] == 1 else gate_ref.shape[1]
            for u in range(wide // span):
                lanes = slice(u * span, (u + 1) * span)
                summed = part[b, c, :, lanes].astype(jnp.float32)
                for o in range(1, heads):
                    summed = summed + got[o - 1, cb, c, :, lanes].astype(jnp.float32)
                at = cb * cols + c * wide + u * span
                gate = gate_ref[:, at:at + span] if span == wide else gate_ref[at // span:at // span + 1, :]
                out_ref[:, at:at + span] = (gate * summed).astype(out_ref.dtype)

    for copy in kv_copies:
        copy.wait_send()
    if fold:
        @pl.when(is_end)
        def _():
            for copy in out_copies:
                copy.wait_send()

        @pl.when(is_helper)
        def _():
            for copy in back_copies:
                copy.wait_send()
    for c in range(pieces):
        @pl.when(t < n - 1)
        def _(c=c):
            first_send(c, 1).wait_send()
        @pl.when(t > 0)
        def _(c=c):
            first_send(c, 0).wait_send()

    def drain(b, carry):
        for c in range(pieces):
            @pl.when(b != t)
            def _(c=c):
                for o in range(1, groups):
                    across(b, c, o).wait_send()
            @pl.when((b < t) & (t < n - 1))
            def _(c=c):
                relay(b, c, 1).wait_send()
            @pl.when((b > t) & (t > 0))
            def _(c=c):
                relay(b, c, 0).wait_send()
            @pl.when(b // per_head != me)
            def _(c=c):
                term_send(b, c, 1).wait_send()
        return carry

    lax.fori_loop(0, n, drain, 0)


def shards(queries, key_rows, value_rows, keep_tiles, out_weight, gate_scale):
    n, heads, groups = lax.axis_size("tm"), lax.axis_size("head"), lax.axis_size("groups")
    reach = min(2, (n - 1) // 2)
    tokens = queries.shape[0]
    head_count = queries.shape[1]
    flat = head_count * HD
    rows, cols = out_weight.shape
    pieces = cols // 256 if cols % 256 == 0 else 1
    wide = cols // pieces
    per_head = n // heads
    slabs = 2 * reach + 1
    gate_lanes = 128 if wide % 128 == 0 else gate_scale.shape[0]
    vmem = pl.BlockSpec(memory_space=pltpu.VMEM)
    hbm = pl.BlockSpec(memory_space=pl.ANY)
    dma = pltpu.SemaphoreType.DMA
    bf16 = jnp.bfloat16
    return pl.pallas_call(
        functools.partial(layer_kernel, (groups, n, heads, reach, pieces)),
        out_shape=jax.ShapeDtypeStruct((tokens, gate_scale.shape[0]), bf16),
        in_specs=[hbm, hbm, hbm, pl.BlockSpec(memory_space=pltpu.SMEM), hbm, vmem],
        out_specs=vmem,
        scratch_shapes=[
            pltpu.VMEM((head_count, tokens, HD), bf16),
            pltpu.VMEM((slabs + 1, head_count, tokens, HD), bf16),
            pltpu.VMEM((slabs + 1, head_count, tokens, HD), bf16),
            pltpu.VMEM((n, pieces, rows, wide), bf16),
            pltpu.VMEM((tokens, flat), bf16),
            pltpu.VMEM((n, pieces, tokens, wide), bf16),
            pltpu.VMEM((heads - 1, per_head, pieces, tokens, wide), bf16),
            dma((slabs, 2)),
            dma((slabs + 1, 2)),
            dma((2, n, pieces)),
            dma((n, pieces)),
            dma((groups - 1, n, pieces)),
            dma((groups - 1, n, pieces)),
            dma((n, pieces)),
            dma((heads - 1, per_head, pieces)),
            dma((pieces,)),
            dma((5,)),
            pltpu.VMEM((head_count, tokens, HD), bf16),
            pltpu.VMEM((head_count, tokens, HD), bf16),
            pltpu.VMEM((head_count, tokens, HD), bf16),
            pltpu.VMEM((8, tokens), jnp.float32),
            pltpu.VMEM((8, tokens), jnp.float32),
            pltpu.VMEM((tokens, 128), jnp.float32),
            pltpu.VMEM((tokens, 128), jnp.float32),
            pltpu.VMEM((tokens, 128), jnp.float32),
            dma((4,)),
            dma((4,)),
        ],
        compiler_params=pltpu.CompilerParams(
            collective_id=0, has_side_effects=True, vmem_limit_bytes=56 * 1024 * 1024
        ),
    )(
        queries.transpose(1, 0, 2),
        key_rows.transpose(1, 0, 2),
        value_rows.transpose(1, 0, 2),
        keep_tiles,
        out_weight,
        gate_scale.reshape(-1, gate_lanes),
    )


def solution(mesh):
    placed = (
        P(("groups", "tm"), "head", None),
        P(("groups", "tm"), "head", None),
        P(("groups", "tm"), "head", None),
        P(("groups", "tm"), None),
        P("head", "tm"),
        P(("groups", "head")),
    )
    return jax.shard_map(
        shards, mesh=mesh, in_specs=placed, out_specs=P(("groups", "tm"), "head"), check_vma=False
    )
```

```python
import functools
import math

import jax
import jax.numpy as jnp
from jax import lax
from jax.experimental import pallas as pl
from jax.experimental.pallas import tpu as pltpu
from jax.sharding import PartitionSpec as P

HD = 128
TILE = 128
MESH = pl.DeviceIdType.MESH


def layer_kernel(
    sizes, q_ref, k_ref, v_ref, keep_ref, w_ref, gate_ref, out_ref,
    q_own, k_all, v_all, w_all, attended, part, got,
    kv_send, kv_recv, z_send, z_recv, y_send, y_recv, r_send, r_recv, own_sem, in_sem,
):
    groups, n, heads, reach, pieces = sizes
    g, t, me = lax.axis_index("groups"), lax.axis_index("tm"), lax.axis_index("head")
    rows, cols = w_ref.shape
    wide = cols // pieces
    per_head = n // heads
    part_rows = rows // groups
    head_count, tokens = q_ref.shape[0], q_ref.shape[1]
    slabs = 2 * reach + 1

    barrier = pltpu.get_barrier_semaphore()
    partners = []
    for d in range(1, reach + 1):
        partners += [{"tm": lax.rem(t + d, n)}, {"tm": lax.rem(t + n - d, n)}]
    for o in range(1, groups):
        partners.append({"groups": lax.rem(g + o, groups)})
    for o in range(1, heads):
        partners.append({"head": lax.rem(me + o, heads)})
    for partner in partners:
        pl.semaphore_signal(barrier, inc=1, device_id=partner, device_id_type=MESH)
    pl.semaphore_wait(barrier, len(partners))

    def remote(src, dst, send, recv, device):
        return pltpu.make_async_remote_copy(
            src_ref=src, dst_ref=dst, send_sem=send, recv_sem=recv,
            device_id=device, device_id_type=MESH,
        )

    kv_copies = []
    for d in range(1, reach + 1):
        for slot, to in ((reach - d, lax.rem(t + d, n)), (reach + d, lax.rem(t + n - d, n))):
            for which, (src, dst) in enumerate(((k_ref, k_all), (v_ref, v_all))):
                kv_copies.append(
                    remote(src, dst.at[slot], kv_send.at[slot, which], kv_recv.at[slot, which], {"tm": to})
                )
    for copy in kv_copies:
        copy.start()
    in_copies = [
        pltpu.make_async_copy(src, dst, in_sem.at[i])
        for i, (src, dst) in enumerate(
            ((q_ref, q_own), (k_ref, k_all.at[reach]), (v_ref, v_all.at[reach]))
        )
    ]
    for copy in in_copies:
        copy.start()

    my_rows = pl.ds(pl.multiple_of(g * part_rows, part_rows), part_rows)

    def own_copy(c):
        return pltpu.make_async_copy(
            w_ref.at[:, c * wide:(c + 1) * wide], w_all.at[t, c], own_sem.at[c]
        )

    def first_send(c, side):
        to = jnp.minimum(t + 1, n - 1) if side else jnp.maximum(t - 1, 0)
        return remote(
            w_ref.at[my_rows, c * wide:(c + 1) * wide], w_all.at[t, c, my_rows],
            z_send.at[side, t, c], z_recv.at[t, c], {"tm": to},
        )

    def relay(b, c, side):
        to = jnp.minimum(t + 1, n - 1) if side else jnp.maximum(t - 1, 0)
        return remote(
            w_all.at[b, c, my_rows], w_all.at[b, c, my_rows],
            z_send.at[side, b, c], z_recv.at[b, c], {"tm": to},
        )

    def across(b, c, o):
        return remote(
            w_all.at[b, c, my_rows], w_all.at[b, c, my_rows],
            y_send.at[o - 1, b, c], y_recv.at[o - 1, b, c],
            {"groups": lax.rem(g + o, groups)},
        )

    def across_arrival(b, c, o):
        sender = lax.rem(g + groups - o, groups)
        their_rows = pl.ds(pl.multiple_of(sender * part_rows, part_rows), part_rows)
        return remote(
            w_all.at[b, c, their_rows], w_all.at[b, c, their_rows],
            y_send.at[o - 1, b, c], y_recv.at[o - 1, b, c],
            {"groups": lax.rem(g + o, groups)},
        )

    def term_send(b, c, o):
        return remote(
            part.at[b, c], got.at[o - 1, b % per_head, c],
            r_send.at[b, c], r_recv.at[o - 1, b % per_head, c],
            {"head": lax.rem(me + o, heads)},
        )

    for c in range(pieces):
        own_copy(c).start()
        @pl.when(t < n - 1)
        def _(c=c):
            first_send(c, 1).start()
        @pl.when(t > 0)
        def _(c=c):
            first_send(c, 0).start()

    for copy in in_copies:
        copy.wait()
    for copy in kv_copies:
        copy.wait_recv()

    scale = 1.0 / math.sqrt(HD)
    per_slab = tokens // TILE

    early = min(pieces, head_count - 1)

    def pass_on(j, side):
        step, c = j // pieces, j % pieces
        b = (t - 1 - step) if side else (t + 1 + step)
        @pl.when((b >= 0) & (b <= n - 1))
        def _():
            relay(b, c, side).wait_recv()
            @pl.when((t < n - 1) if side else (t > 0))
            def _():
                relay(b, c, side).start()
            for o in range(1, groups):
                across(b, c, o).start()

    def one_head(h, carry):
        lanes = pl.ds(pl.multiple_of(h * HD, HD), HD)
        for i in range(per_slab):
            q = q_own[h, i * TILE:(i + 1) * TILE, :]
            scores = []
            for j in range(slabs):
                s = lax.dot_general(
                    q, k_all[j, h], (((1,), (1,)), ((), ())), preferred_element_type=jnp.float32
                )
                bias = jnp.concatenate(
                    [
                        jnp.full(
                            (1, TILE),
                            jnp.where(keep_ref[i, j * per_slab + u] > 0, 0.0, -jnp.inf),
                            jnp.float32,
                        )
                        for u in range(per_slab)
                    ],
                    axis=1,
                )
                scores.append(s * scale + bias)
            peak = functools.reduce(
                jnp.maximum, [jnp.max(s, axis=1, keepdims=True) for s in scores]
            )
            exps = [jnp.exp(s - peak) for s in scores]
            total = functools.reduce(jnp.add, [jnp.sum(e, axis=1, keepdims=True) for e in exps])
            inverse = 1.0 / total
            acc = None
            for j in range(slabs):
                term = jnp.dot(
                    (exps[j] * inverse).astype(jnp.bfloat16), v_all[j, h],
                    preferred_element_type=jnp.float32,
                )
                acc = term if acc is None else acc + term
            attended[i * TILE:(i + 1) * TILE, lanes] = acc.astype(jnp.bfloat16)
        @pl.when(h >= head_count - early)
        def _():
            for side in (1, 0):
                pass_on(h - (head_count - early), side)
        return carry

    lax.fori_loop(0, head_count, one_head, 0)

    def project(b, c):
        def tile(i, carry):
            at = pl.ds(pl.multiple_of(i * TILE, TILE), TILE)
            part[b, c, at, :] = jnp.dot(
                attended[at, :], w_all[b, c], preferred_element_type=jnp.float32
            ).astype(jnp.bfloat16)
            return carry

        lax.fori_loop(0, tokens // TILE, tile, 0)
        owner = b // per_head
        for o in range(1, heads):
            @pl.when(owner == lax.rem(me + o, heads))
            def _():
                term_send(b, c, o).start()

    for c in range(pieces):
        own_copy(c).wait()
        project(t, c)

    def use(j, side):
        step, c = j // pieces, j % pieces
        b = (t - 1 - step) if side else (t + 1 + step)
        @pl.when((b >= 0) & (b <= n - 1))
        def _():
            for o in range(1, groups):
                across_arrival(b, c, o).wait_recv()
            project(b, c)

    def step(j, carry):
        @pl.when(j >= early)
        def _():
            for side in (1, 0):
                pass_on(j, side)
        @pl.when(j > 0)
        def _():
            for side in (1, 0):
                use(j - 1, side)
        return carry

    count = (n - 1) * pieces
    lax.fori_loop(0, count, step, 0)
    for side in (1, 0):
        use(count - 1, side)

    for cb in range(per_head):
        for c in range(pieces):
            b = me * per_head + cb
            for o in range(1, heads):
                term_send(b, c, o).wait_recv()
            span = wide if gate_ref.shape[0] == 1 else gate_ref.shape[1]
            for u in range(wide // span):
                lanes = slice(u * span, (u + 1) * span)
                summed = part[b, c, :, lanes].astype(jnp.float32)
                for o in range(1, heads):
                    summed = summed + got[o - 1, cb, c, :, lanes].astype(jnp.float32)
                at = cb * cols + c * wide + u * span
                gate = gate_ref[:, at:at + span] if gate_ref.shape[0] == 1 else gate_ref[at // span:at // span + 1, :]
                out_ref[:, at:at + span] = (gate * summed).astype(out_ref.dtype)

    for copy in kv_copies:
        copy.wait_send()
    for c in range(pieces):
        @pl.when(t < n - 1)
        def _(c=c):
            first_send(c, 1).wait_send()
        @pl.when(t > 0)
        def _(c=c):
            first_send(c, 0).wait_send()

    def drain(b, carry):
        for c in range(pieces):
            @pl.when(b != t)
            def _(c=c):
                for o in range(1, groups):
                    across(b, c, o).wait_send()
            @pl.when((b < t) & (t < n - 1))
            def _(c=c):
                relay(b, c, 1).wait_send()
            @pl.when((b > t) & (t > 0))
            def _(c=c):
                relay(b, c, 0).wait_send()
            @pl.when(b // per_head != me)
            def _(c=c):
                term_send(b, c, 1).wait_send()
        return carry

    lax.fori_loop(0, n, drain, 0)


def shards(queries, key_rows, value_rows, keep_tiles, out_weight, gate_scale):
    n, heads, groups = lax.axis_size("tm"), lax.axis_size("head"), lax.axis_size("groups")
    reach = min(2, (n - 1) // 2)
    tokens = queries.shape[0]
    head_count = queries.shape[1]
    flat = head_count * HD
    rows, cols = out_weight.shape
    pieces = cols // 128 if cols % 128 == 0 else 1
    wide = cols // pieces
    per_head = n // heads
    slabs = 2 * reach + 1
    gate_lanes = 128 if wide % 128 == 0 else gate_scale.shape[0]
    vmem = pl.BlockSpec(memory_space=pltpu.VMEM)
    hbm = pl.BlockSpec(memory_space=pl.ANY)
    dma = pltpu.SemaphoreType.DMA
    bf16 = jnp.bfloat16
    return pl.pallas_call(
        functools.partial(layer_kernel, (groups, n, heads, reach, pieces)),
        out_shape=jax.ShapeDtypeStruct((tokens, gate_scale.shape[0]), bf16),
        in_specs=[hbm, hbm, hbm, pl.BlockSpec(memory_space=pltpu.SMEM), hbm, vmem],
        out_specs=vmem,
        scratch_shapes=[
            pltpu.VMEM((head_count, tokens, HD), bf16),
            pltpu.VMEM((slabs, head_count, tokens, HD), bf16),
            pltpu.VMEM((slabs, head_count, tokens, HD), bf16),
            pltpu.VMEM((n, pieces, rows, wide), bf16),
            pltpu.VMEM((tokens, flat), bf16),
            pltpu.VMEM((n, pieces, tokens, wide), bf16),
            pltpu.VMEM((heads - 1, per_head, pieces, tokens, wide), bf16),
            dma((slabs, 2)),
            dma((slabs, 2)),
            dma((2, n, pieces)),
            dma((n, pieces)),
            dma((groups - 1, n, pieces)),
            dma((groups - 1, n, pieces)),
            dma((n, pieces)),
            dma((heads - 1, per_head, pieces)),
            dma((pieces,)),
            dma((3,)),
        ],
        compiler_params=pltpu.CompilerParams(
            collective_id=0, has_side_effects=True, vmem_limit_bytes=56 * 1024 * 1024
        ),
    )(
        queries.transpose(1, 0, 2),
        key_rows.transpose(1, 0, 2),
        value_rows.transpose(1, 0, 2),
        keep_tiles,
        out_weight,
        gate_scale.reshape(-1, gate_lanes),
    )


def solution(mesh):
    placed = (
        P(("groups", "tm"), "head", None),
        P(("groups", "tm"), "head", None),
        P(("groups", "tm"), "head", None),
        P(("groups", "tm"), None),
        P("head", "tm"),
        P(("groups", "head")),
    )
    return jax.shard_map(
        shards, mesh=mesh, in_specs=placed, out_specs=P(("groups", "tm"), "head"), check_vma=False
    )
```

```python
import functools
import math

import jax
import jax.numpy as jnp
from jax import lax
from jax.experimental import pallas as pl
from jax.experimental.pallas import tpu as pltpu
from jax.sharding import PartitionSpec as P

HD = 128
TILE = 128
MESH = pl.DeviceIdType.MESH


def layer_kernel(
    sizes, q_ref, k_ref, v_ref, keep_ref, w_ref, gate_ref, out_ref,
    q_own, k_all, v_all, w_all, attended, part, got,
    kv_send, kv_recv, z_send, z_recv, y_send, y_recv, r_send, r_recv, own_sem, in_sem,
):
    groups, n, heads, reach, pieces = sizes
    g, t, me = lax.axis_index("groups"), lax.axis_index("tm"), lax.axis_index("head")
    rows, cols = w_ref.shape
    wide = cols // pieces
    per_head = n // heads
    part_rows = rows // groups
    head_count, tokens = q_ref.shape[0], q_ref.shape[1]
    slabs = 2 * reach + 1

    barrier = pltpu.get_barrier_semaphore()
    partners = []
    for d in range(1, reach + 1):
        partners += [{"tm": lax.rem(t + d, n)}, {"tm": lax.rem(t + n - d, n)}]
    for o in range(1, groups):
        partners.append({"groups": lax.rem(g + o, groups)})
    for o in range(1, heads):
        partners.append({"head": lax.rem(me + o, heads)})
    for partner in partners:
        pl.semaphore_signal(barrier, inc=1, device_id=partner, device_id_type=MESH)
    pl.semaphore_wait(barrier, len(partners))

    def remote(src, dst, send, recv, device):
        return pltpu.make_async_remote_copy(
            src_ref=src, dst_ref=dst, send_sem=send, recv_sem=recv,
            device_id=device, device_id_type=MESH,
        )

    kv_copies = []
    for d in range(1, reach + 1):
        for slot, to in ((reach - d, lax.rem(t + d, n)), (reach + d, lax.rem(t + n - d, n))):
            for which, (src, dst) in enumerate(((k_ref, k_all), (v_ref, v_all))):
                kv_copies.append(
                    remote(src, dst.at[slot], kv_send.at[slot, which], kv_recv.at[slot, which], {"tm": to})
                )
    for copy in kv_copies:
        copy.start()
    in_copies = [
        pltpu.make_async_copy(src, dst, in_sem.at[i])
        for i, (src, dst) in enumerate(
            ((q_ref, q_own), (k_ref, k_all.at[reach]), (v_ref, v_all.at[reach]))
        )
    ]
    for copy in in_copies:
        copy.start()

    my_rows = pl.ds(pl.multiple_of(g * part_rows, part_rows), part_rows)

    def own_copy(c):
        return pltpu.make_async_copy(
            w_ref.at[:, c * wide:(c + 1) * wide], w_all.at[t, c], own_sem.at[c]
        )

    def first_send(c, side):
        to = jnp.minimum(t + 1, n - 1) if side else jnp.maximum(t - 1, 0)
        return remote(
            w_ref.at[my_rows, c * wide:(c + 1) * wide], w_all.at[t, c, my_rows],
            z_send.at[side, t, c], z_recv.at[t, c], {"tm": to},
        )

    def relay(b, c, side):
        to = jnp.minimum(t + 1, n - 1) if side else jnp.maximum(t - 1, 0)
        return remote(
            w_all.at[b, c, my_rows], w_all.at[b, c, my_rows],
            z_send.at[side, b, c], z_recv.at[b, c], {"tm": to},
        )

    def across(b, c, o):
        return remote(
            w_all.at[b, c, my_rows], w_all.at[b, c, my_rows],
            y_send.at[o - 1, b, c], y_recv.at[o - 1, b, c],
            {"groups": lax.rem(g + o, groups)},
        )

    def across_arrival(b, c, o):
        sender = lax.rem(g + groups - o, groups)
        their_rows = pl.ds(pl.multiple_of(sender * part_rows, part_rows), part_rows)
        return remote(
            w_all.at[b, c, their_rows], w_all.at[b, c, their_rows],
            y_send.at[o - 1, b, c], y_recv.at[o - 1, b, c],
            {"groups": lax.rem(g + o, groups)},
        )

    def term_send(b, c, o):
        return remote(
            part.at[b, c], got.at[o - 1, b % per_head, c],
            r_send.at[b, c], r_recv.at[o - 1, b % per_head, c],
            {"head": lax.rem(me + o, heads)},
        )

    for c in range(pieces):
        own_copy(c).start()
        @pl.when(t < n - 1)
        def _(c=c):
            first_send(c, 1).start()
        @pl.when(t > 0)
        def _(c=c):
            first_send(c, 0).start()

    for copy in in_copies:
        copy.wait()
    for copy in kv_copies:
        copy.wait_recv()

    scale = 1.0 / math.sqrt(HD)
    per_slab = tokens // TILE

    early = min(pieces, head_count - 1)

    def pass_on(j, side):
        step, c = j // pieces, j % pieces
        b = (t - 1 - step) if side else (t + 1 + step)
        @pl.when((b >= 0) & (b <= n - 1))
        def _():
            relay(b, c, side).wait_recv()
            @pl.when((t < n - 1) if side else (t > 0))
            def _():
                relay(b, c, side).start()
            for o in range(1, groups):
                across(b, c, o).start()

    def one_head(h, carry):
        lanes = pl.ds(pl.multiple_of(h * HD, HD), HD)
        for i in range(per_slab):
            q = q_own[h, i * TILE:(i + 1) * TILE, :]
            scores = []
            for j in range(slabs):
                s = lax.dot_general(
                    q, k_all[j, h], (((1,), (1,)), ((), ())), preferred_element_type=jnp.float32
                )
                bias = jnp.concatenate(
                    [
                        jnp.full(
                            (1, TILE),
                            jnp.where(keep_ref[i, j * per_slab + u] > 0, 0.0, -jnp.inf),
                            jnp.float32,
                        )
                        for u in range(per_slab)
                    ],
                    axis=1,
                )
                scores.append(s * scale + bias)
            peak = functools.reduce(
                jnp.maximum, [jnp.max(s, axis=1, keepdims=True) for s in scores]
            )
            exps = [jnp.exp(s - peak) for s in scores]
            total = functools.reduce(jnp.add, [jnp.sum(e, axis=1, keepdims=True) for e in exps])
            inverse = 1.0 / total
            acc = None
            for j in range(slabs):
                term = jnp.dot(
                    (exps[j] * inverse).astype(jnp.bfloat16), v_all[j, h],
                    preferred_element_type=jnp.float32,
                )
                acc = term if acc is None else acc + term
            attended[i * TILE:(i + 1) * TILE, lanes] = acc.astype(jnp.bfloat16)
        @pl.when(h >= head_count - early)
        def _():
            for side in (1, 0):
                pass_on(h - (head_count - early), side)
        return carry

    lax.fori_loop(0, head_count, one_head, 0)

    def project(b, c):
        def tile(i, carry):
            at = pl.ds(pl.multiple_of(i * TILE, TILE), TILE)
            part[b, c, at, :] = jnp.dot(
                attended[at, :], w_all[b, c], preferred_element_type=jnp.float32
            ).astype(jnp.bfloat16)
            return carry

        lax.fori_loop(0, tokens // TILE, tile, 0)
        owner = b // per_head
        for o in range(1, heads):
            @pl.when(owner == lax.rem(me + o, heads))
            def _():
                term_send(b, c, o).start()

    for c in range(pieces):
        own_copy(c).wait()
        project(t, c)

    def use(j, side):
        step, c = j // pieces, j % pieces
        b = (t - 1 - step) if side else (t + 1 + step)
        @pl.when((b >= 0) & (b <= n - 1))
        def _():
            for o in range(1, groups):
                across_arrival(b, c, o).wait_recv()
            project(b, c)

    count = (n - 1) * pieces

    def use_both(j, carry):
        for side in (1, 0):
            use(j, side)
        return carry

    def step(j, carry):
        for side in (1, 0):
            pass_on(j, side)
        first = jnp.minimum(2 * (j - early), j - 1)
        last = jnp.minimum(2 * (j - early) + 2, j)
        return lax.fori_loop(first, last, use_both, carry)

    lax.fori_loop(early, count, step, 0)
    lax.fori_loop(min(2 * (count - early), count - 1), count, use_both, 0)

    for cb in range(per_head):
        for c in range(pieces):
            b = me * per_head + cb
            for o in range(1, heads):
                term_send(b, c, o).wait_recv()
            span = wide if gate_ref.shape[0] == 1 else gate_ref.shape[1]
            for u in range(wide // span):
                lanes = slice(u * span, (u + 1) * span)
                summed = part[b, c, :, lanes].astype(jnp.float32)
                for o in range(1, heads):
                    summed = summed + got[o - 1, cb, c, :, lanes].astype(jnp.float32)
                at = cb * cols + c * wide + u * span
                gate = gate_ref[:, at:at + span] if span == wide else gate_ref[at // span:at // span + 1, :]
                out_ref[:, at:at + span] = (gate * summed).astype(out_ref.dtype)

    for copy in kv_copies:
        copy.wait_send()
    for c in range(pieces):
        @pl.when(t < n - 1)
        def _(c=c):
            first_send(c, 1).wait_send()
        @pl.when(t > 0)
        def _(c=c):
            first_send(c, 0).wait_send()

    def drain(b, carry):
        for c in range(pieces):
            @pl.when(b != t)
            def _(c=c):
                for o in range(1, groups):
                    across(b, c, o).wait_send()
            @pl.when((b < t) & (t < n - 1))
            def _(c=c):
                relay(b, c, 1).wait_send()
            @pl.when((b > t) & (t > 0))
            def _(c=c):
                relay(b, c, 0).wait_send()
            @pl.when(b // per_head != me)
            def _(c=c):
                term_send(b, c, 1).wait_send()
        return carry

    lax.fori_loop(0, n, drain, 0)


def shards(queries, key_rows, value_rows, keep_tiles, out_weight, gate_scale):
    n, heads, groups = lax.axis_size("tm"), lax.axis_size("head"), lax.axis_size("groups")
    reach = min(2, (n - 1) // 2)
    tokens = queries.shape[0]
    head_count = queries.shape[1]
    flat = head_count * HD
    rows, cols = out_weight.shape
    pieces = cols // 256 if cols % 256 == 0 else 1
    wide = cols // pieces
    per_head = n // heads
    slabs = 2 * reach + 1
    gate_lanes = 128 if wide % 128 == 0 else gate_scale.shape[0]
    vmem = pl.BlockSpec(memory_space=pltpu.VMEM)
    hbm = pl.BlockSpec(memory_space=pl.ANY)
    dma = pltpu.SemaphoreType.DMA
    bf16 = jnp.bfloat16
    return pl.pallas_call(
        functools.partial(layer_kernel, (groups, n, heads, reach, pieces)),
        out_shape=jax.ShapeDtypeStruct((tokens, gate_scale.shape[0]), bf16),
        in_specs=[hbm, hbm, hbm, pl.BlockSpec(memory_space=pltpu.SMEM), hbm, vmem],
        out_specs=vmem,
        scratch_shapes=[
            pltpu.VMEM((head_count, tokens, HD), bf16),
            pltpu.VMEM((slabs, head_count, tokens, HD), bf16),
            pltpu.VMEM((slabs, head_count, tokens, HD), bf16),
            pltpu.VMEM((n, pieces, rows, wide), bf16),
            pltpu.VMEM((tokens, flat), bf16),
            pltpu.VMEM((n, pieces, tokens, wide), bf16),
            pltpu.VMEM((heads - 1, per_head, pieces, tokens, wide), bf16),
            dma((slabs, 2)),
            dma((slabs, 2)),
            dma((2, n, pieces)),
            dma((n, pieces)),
            dma((groups - 1, n, pieces)),
            dma((groups - 1, n, pieces)),
            dma((n, pieces)),
            dma((heads - 1, per_head, pieces)),
            dma((pieces,)),
            dma((3,)),
        ],
        compiler_params=pltpu.CompilerParams(
            collective_id=0, has_side_effects=True, vmem_limit_bytes=56 * 1024 * 1024
        ),
    )(
        queries.transpose(1, 0, 2),
        key_rows.transpose(1, 0, 2),
        value_rows.transpose(1, 0, 2),
        keep_tiles,
        out_weight,
        gate_scale.reshape(-1, gate_lanes),
    )


def solution(mesh):
    placed = (
        P(("groups", "tm"), "head", None),
        P(("groups", "tm"), "head", None),
        P(("groups", "tm"), "head", None),
        P(("groups", "tm"), None),
        P("head", "tm"),
        P(("groups", "head")),
    )
    return jax.shard_map(
        shards, mesh=mesh, in_specs=placed, out_specs=P(("groups", "tm"), "head"), check_vma=False
    )
```

```python
import functools
import math

import jax
import jax.numpy as jnp
from jax import lax
from jax.experimental import pallas as pl
from jax.experimental.pallas import tpu as pltpu
from jax.sharding import PartitionSpec as P

HD = 128
TILE = 128
MESH = pl.DeviceIdType.MESH


def layer_kernel(
    sizes, q_ref, k_ref, v_ref, keep_ref, w_ref, gate_ref, out_ref,
    q_own, k_all, v_all, w_all, attended, part, got,
    kv_send, kv_recv, z_send, z_recv, y_send, y_recv, r_send, r_recv, own_sem, in_sem,
):
    groups, n, heads, reach, pieces = sizes
    g, t, me = lax.axis_index("groups"), lax.axis_index("tm"), lax.axis_index("head")
    rows, cols = w_ref.shape
    wide = cols // pieces
    per_head = n // heads
    part_rows = rows // groups
    head_count, tokens = q_ref.shape[0], q_ref.shape[1]
    slabs = 2 * reach + 1

    barrier = pltpu.get_barrier_semaphore()
    partners = []
    for d in range(1, reach + 1):
        partners += [{"tm": lax.rem(t + d, n)}, {"tm": lax.rem(t + n - d, n)}]
    for o in range(1, groups):
        partners.append({"groups": lax.rem(g + o, groups)})
    for o in range(1, heads):
        partners.append({"head": lax.rem(me + o, heads)})
    for partner in partners:
        pl.semaphore_signal(barrier, inc=1, device_id=partner, device_id_type=MESH)
    pl.semaphore_wait(barrier, len(partners))

    def remote(src, dst, send, recv, device):
        return pltpu.make_async_remote_copy(
            src_ref=src, dst_ref=dst, send_sem=send, recv_sem=recv,
            device_id=device, device_id_type=MESH,
        )

    kv_copies = []
    for d in range(1, reach + 1):
        for slot, to in ((reach - d, lax.rem(t + d, n)), (reach + d, lax.rem(t + n - d, n))):
            for which, (src, dst) in enumerate(((k_ref, k_all), (v_ref, v_all))):
                kv_copies.append(
                    remote(src, dst.at[slot], kv_send.at[slot, which], kv_recv.at[slot, which], {"tm": to})
                )
    @pl.when(t == 0)
    def _():
        for copy in reversed(kv_copies):
            copy.start()

    @pl.when(t != 0)
    def _():
        for copy in kv_copies:
            copy.start()

    in_copies = [
        pltpu.make_async_copy(src, dst, in_sem.at[i])
        for i, (src, dst) in enumerate(
            ((q_ref, q_own), (k_ref, k_all.at[reach]), (v_ref, v_all.at[reach]))
        )
    ]
    for copy in in_copies:
        copy.start()

    my_rows = pl.ds(pl.multiple_of(g * part_rows, part_rows), part_rows)

    def own_copy(c):
        return pltpu.make_async_copy(
            w_ref.at[:, c * wide:(c + 1) * wide], w_all.at[t, c], own_sem.at[c]
        )

    def first_send(c, side):
        to = jnp.minimum(t + 1, n - 1) if side else jnp.maximum(t - 1, 0)
        return remote(
            w_ref.at[my_rows, c * wide:(c + 1) * wide], w_all.at[t, c, my_rows],
            z_send.at[side, t, c], z_recv.at[t, c], {"tm": to},
        )

    def relay(b, c, side):
        to = jnp.minimum(t + 1, n - 1) if side else jnp.maximum(t - 1, 0)
        return remote(
            w_all.at[b, c, my_rows], w_all.at[b, c, my_rows],
            z_send.at[side, b, c], z_recv.at[b, c], {"tm": to},
        )

    def across(b, c, o):
        return remote(
            w_all.at[b, c, my_rows], w_all.at[b, c, my_rows],
            y_send.at[o - 1, b, c], y_recv.at[o - 1, b, c],
            {"groups": lax.rem(g + o, groups)},
        )

    def across_arrival(b, c, o):
        sender = lax.rem(g + groups - o, groups)
        their_rows = pl.ds(pl.multiple_of(sender * part_rows, part_rows), part_rows)
        return remote(
            w_all.at[b, c, their_rows], w_all.at[b, c, their_rows],
            y_send.at[o - 1, b, c], y_recv.at[o - 1, b, c],
            {"groups": lax.rem(g + o, groups)},
        )

    def term_send(b, c, o):
        return remote(
            part.at[b, c], got.at[o - 1, b % per_head, c],
            r_send.at[b, c], r_recv.at[o - 1, b % per_head, c],
            {"head": lax.rem(me + o, heads)},
        )

    for c in range(pieces):
        own_copy(c).start()
        @pl.when(t < n - 1)
        def _(c=c):
            first_send(c, 1).start()
        @pl.when(t > 0)
        def _(c=c):
            first_send(c, 0).start()

    for copy in in_copies:
        copy.wait()
    for copy in kv_copies:
        copy.wait_recv()

    scale = 1.0 / math.sqrt(HD)
    per_slab = tokens // TILE

    early = min(pieces, head_count - 1)

    def pass_on(j, side):
        step, c = j // pieces, j % pieces
        b = (t - 1 - step) if side else (t + 1 + step)
        @pl.when((b >= 0) & (b <= n - 1))
        def _():
            relay(b, c, side).wait_recv()
            @pl.when((t < n - 1) if side else (t > 0))
            def _():
                relay(b, c, side).start()
            for o in range(1, groups):
                across(b, c, o).start()

    def one_head(h, carry):
        lanes = pl.ds(pl.multiple_of(h * HD, HD), HD)
        for i in range(per_slab):
            q = q_own[h, i * TILE:(i + 1) * TILE, :]
            scores = []
            for j in range(slabs):
                s = lax.dot_general(
                    q, k_all[j, h], (((1,), (1,)), ((), ())), preferred_element_type=jnp.float32
                )
                bias = jnp.concatenate(
                    [
                        jnp.full(
                            (1, TILE),
                            jnp.where(keep_ref[i, j * per_slab + u] > 0, 0.0, -jnp.inf),
                            jnp.float32,
                        )
                        for u in range(per_slab)
                    ],
                    axis=1,
                )
                scores.append(s * scale + bias)
            peak = functools.reduce(
                jnp.maximum, [jnp.max(s, axis=1, keepdims=True) for s in scores]
            )
            exps = [jnp.exp(s - peak) for s in scores]
            total = functools.reduce(jnp.add, [jnp.sum(e, axis=1, keepdims=True) for e in exps])
            inverse = 1.0 / total
            acc = None
            for j in range(slabs):
                term = jnp.dot(
                    (exps[j] * inverse).astype(jnp.bfloat16), v_all[j, h],
                    preferred_element_type=jnp.float32,
                )
                acc = term if acc is None else acc + term
            attended[i * TILE:(i + 1) * TILE, lanes] = acc.astype(jnp.bfloat16)
        @pl.when(h >= head_count - early)
        def _():
            for side in (1, 0):
                pass_on(h - (head_count - early), side)
        return carry

    lax.fori_loop(0, head_count, one_head, 0)

    def project(b, c):
        def tile(i, carry):
            at = pl.ds(pl.multiple_of(i * TILE, TILE), TILE)
            part[b, c, at, :] = jnp.dot(
                attended[at, :], w_all[b, c], preferred_element_type=jnp.float32
            ).astype(jnp.bfloat16)
            return carry

        lax.fori_loop(0, tokens // TILE, tile, 0)
        owner = b // per_head
        for o in range(1, heads):
            @pl.when(owner == lax.rem(me + o, heads))
            def _():
                term_send(b, c, o).start()

    for c in range(pieces):
        own_copy(c).wait()
        project(t, c)

    def use(j, side):
        step, c = j // pieces, j % pieces
        b = (t - 1 - step) if side else (t + 1 + step)
        @pl.when((b >= 0) & (b <= n - 1))
        def _():
            for o in range(1, groups):
                across_arrival(b, c, o).wait_recv()
            project(b, c)

    count = (n - 1) * pieces

    def use_both(j, carry):
        for side in (1, 0):
            use(j, side)
        return carry

    def step(j, carry):
        for side in (1, 0):
            pass_on(j, side)
        first = jnp.minimum(2 * (j - early), j - 1)
        last = jnp.minimum(2 * (j - early) + 2, j)
        return lax.fori_loop(first, last, use_both, carry)

    lax.fori_loop(early, count, step, 0)
    lax.fori_loop(min(2 * (count - early), count - 1), count, use_both, 0)

    for cb in range(per_head):
        for c in range(pieces):
            b = me * per_head + cb
            for o in range(1, heads):
                term_send(b, c, o).wait_recv()
            span = wide if gate_ref.shape[0] == 1 else gate_ref.shape[1]
            for u in range(wide // span):
                lanes = slice(u * span, (u + 1) * span)
                summed = part[b, c, :, lanes].astype(jnp.float32)
                for o in range(1, heads):
                    summed = summed + got[o - 1, cb, c, :, lanes].astype(jnp.float32)
                at = cb * cols + c * wide + u * span
                gate = gate_ref[:, at:at + span] if span == wide else gate_ref[at // span:at // span + 1, :]
                out_ref[:, at:at + span] = (gate * summed).astype(out_ref.dtype)

    for copy in kv_copies:
        copy.wait_send()
    for c in range(pieces):
        @pl.when(t < n - 1)
        def _(c=c):
            first_send(c, 1).wait_send()
        @pl.when(t > 0)
        def _(c=c):
            first_send(c, 0).wait_send()

    def drain(b, carry):
        for c in range(pieces):
            @pl.when(b != t)
            def _(c=c):
                for o in range(1, groups):
                    across(b, c, o).wait_send()
            @pl.when((b < t) & (t < n - 1))
            def _(c=c):
                relay(b, c, 1).wait_send()
            @pl.when((b > t) & (t > 0))
            def _(c=c):
                relay(b, c, 0).wait_send()
            @pl.when(b // per_head != me)
            def _(c=c):
                term_send(b, c, 1).wait_send()
        return carry

    lax.fori_loop(0, n, drain, 0)


def shards(queries, key_rows, value_rows, keep_tiles, out_weight, gate_scale):
    n, heads, groups = lax.axis_size("tm"), lax.axis_size("head"), lax.axis_size("groups")
    reach = min(2, (n - 1) // 2)
    tokens = queries.shape[0]
    head_count = queries.shape[1]
    flat = head_count * HD
    rows, cols = out_weight.shape
    pieces = cols // 256 if cols % 256 == 0 else 1
    wide = cols // pieces
    per_head = n // heads
    slabs = 2 * reach + 1
    gate_lanes = 128 if wide % 128 == 0 else gate_scale.shape[0]
    vmem = pl.BlockSpec(memory_space=pltpu.VMEM)
    hbm = pl.BlockSpec(memory_space=pl.ANY)
    dma = pltpu.SemaphoreType.DMA
    bf16 = jnp.bfloat16
    return pl.pallas_call(
        functools.partial(layer_kernel, (groups, n, heads, reach, pieces)),
        out_shape=jax.ShapeDtypeStruct((tokens, gate_scale.shape[0]), bf16),
        in_specs=[hbm, hbm, hbm, pl.BlockSpec(memory_space=pltpu.SMEM), hbm, vmem],
        out_specs=vmem,
        scratch_shapes=[
            pltpu.VMEM((head_count, tokens, HD), bf16),
            pltpu.VMEM((slabs, head_count, tokens, HD), bf16),
            pltpu.VMEM((slabs, head_count, tokens, HD), bf16),
            pltpu.VMEM((n, pieces, rows, wide), bf16),
            pltpu.VMEM((tokens, flat), bf16),
            pltpu.VMEM((n, pieces, tokens, wide), bf16),
            pltpu.VMEM((heads - 1, per_head, pieces, tokens, wide), bf16),
            dma((slabs, 2)),
            dma((slabs, 2)),
            dma((2, n, pieces)),
            dma((n, pieces)),
            dma((groups - 1, n, pieces)),
            dma((groups - 1, n, pieces)),
            dma((n, pieces)),
            dma((heads - 1, per_head, pieces)),
            dma((pieces,)),
            dma((3,)),
        ],
        compiler_params=pltpu.CompilerParams(
            collective_id=0, has_side_effects=True, vmem_limit_bytes=56 * 1024 * 1024
        ),
    )(
        queries.transpose(1, 0, 2),
        key_rows.transpose(1, 0, 2),
        value_rows.transpose(1, 0, 2),
        keep_tiles,
        out_weight,
        gate_scale.reshape(-1, gate_lanes),
    )


def solution(mesh):
    placed = (
        P(("groups", "tm"), "head", None),
        P(("groups", "tm"), "head", None),
        P(("groups", "tm"), "head", None),
        P(("groups", "tm"), None),
        P("head", "tm"),
        P(("groups", "head")),
    )
    return jax.shard_map(
        shards, mesh=mesh, in_specs=placed, out_specs=P(("groups", "tm"), "head"), check_vma=False
    )
```
